128 devices in a mesh: region: 16 (over y_lo, z, core), head: 8 (over y_hi, x).
Axes of the slice: x: 4, y: 4 (y_hi: 2, y_lo: 2; y = y_hi * 2 + y_lo), z: 4, core: 2. Of those that a mesh axis runs over, the one named last changes fastest.
Arguments:
- fine_tokens: float32 [73728, 512], P(('region', 'head')), may hold values from -6 to 6
- fine_shift: int32 [1], replicated, may hold values from 1 to 143
- window_counts: int32 [128], P('region'), may hold values from 36 to 144
- fine_qkv: bfloat16 [512, 1536], replicated, may hold values from -4 to 4
- fine_proj: bfloat16 [512, 512], replicated, may hold values from -0.25 to 0.25
- fine_up: bfloat16 [512, 2048], replicated, may hold values from -0.25 to 0.25
- fine_down: bfloat16 [2048, 512], replicated, may hold values from -0.125 to 0.125
- merge_weight: bfloat16 [2048, 1024], replicated, may hold values from -0.125 to 0.125
- coarse_qkv: bfloat16 [1024, 3072], P('region', 'head'), may hold values from -4 to 4
- coarse_proj: bfloat16 [1024, 1024], P('head', 'region'), may hold values from -0.1875 to 0.1875
- coarse_up: bfloat16 [1024, 4096], P('region', 'head'), may hold values from -0.1875 to 0.1875
- coarse_down: bfloat16 [4096, 1024], P('head', 'region'), may hold values from -0.09375 to 0.09375
- expand_weight: bfloat16 [1024, 2048], replicated, may hold values from -0.1875 to 0.1875
- out_weight: bfloat16 [1024, 512], replicated, may hold values from -0.1875 to 0.1875
Outputs:
- fine_result: float32 [73728, 512], P(('region', 'head'))
The draws below stay inside these ranges and needn't reach their ends.
All inputs are finite; a program needn't handle non-finite values.
Results may differ from the reference program's by a relative error of at most 0.012.
Values may be sent and summed in bfloat16 or wider, within the bound.
No kernel may reach another device: no remote copies, remote signals or barrier semaphores. Data moves between devices by JAX's collectives and lax.ppermute only.
A program may use at most 128 MiB of HBM per device.

```python
import jax
import jax.numpy as jnp
from jax import lax

C = 512
HD = 64
HF = 8
D2 = 1024
HC = 16
FFF = 2048
FFC = 4096
WIN = 144
NTOK = 73728
NCW = 128


def drawn_qkv(key, channels, head_count):
    base = jax.random.normal(jax.random.fold_in(key, 11), (channels, head_count, 3, HD), jnp.float32)
    base = jnp.clip(base, -4.0, 4.0) * channels ** (-0.5)
    base = jnp.clip(base, -4.0, 4.0)
    return base.reshape(channels, head_count * 3 * HD)


def draw_fine_qkv(key, part):
    return drawn_qkv(key, C, HF).astype(jnp.bfloat16)


def draw_coarse_qkv(key, part):
    return drawn_qkv(key, D2, HC).astype(jnp.bfloat16)


def place_ends(entries, key, smallest, top_value):
    spot = [jax.random.randint(jax.random.fold_in(key, axis), (), 0, length) for axis, length in enumerate(entries.shape)]
    widest = entries.shape.index(max(entries.shape))
    neighbour = spot[:widest] + [(spot[widest] + 1) % entries.shape[widest]] + spot[widest + 1:]
    return entries.at[tuple(spot)].set(smallest).at[tuple(neighbour)].set(top_value)


def levels(own_key, shape, shards, least, top_value):
    loudness = 1.0
    for axis_at, shards_of in shards:
        steps = jax.random.uniform(jax.random.fold_in(jax.random.fold_in(own_key, 6), axis_at), (shards_of,), jnp.float32, least / len(shards), top_value / len(shards))
        loudness = loudness * jnp.repeat(jnp.exp(steps), shape[axis_at] // shards_of).reshape((-1,) + (1,) * (len(shape) - 1 - axis_at))
    return loudness


def normal_values(key, shape, deviation, limit, cuts=(), kind=jnp.bfloat16):
    drawn = jax.random.normal(key, shape, jnp.float32) * deviation
    if len(cuts) > 0:
        drawn = levels(key, shape, cuts, -0.22, 0.18) * drawn
    return jnp.clip(drawn, min=-limit, max=limit).astype(kind)


def setup_inputs(seed: int = 0) -> dict:
    keys = jax.random.split(jax.random.key(seed), 15)
    fine_tokens = normal_values(keys[0], (NTOK, C), 1.0, 6.0, ((0, 128),), jnp.float32)
    fine_shift = jax.random.randint(keys[1], (1,), 1, WIN).astype(jnp.int32)
    window_counts = place_ends(jax.random.randint(keys[2], (NCW,), WIN // 4, WIN + 1), jax.random.fold_in(keys[2], 1), WIN // 4, WIN).astype(jnp.int32)
    fine_qkv = draw_fine_qkv(jax.random.fold_in(keys[14], 71), 0)
    fine_proj = normal_values(keys[4], (C, C), C ** -0.5, 0.25)
    fine_up = normal_values(keys[5], (C, FFF), C ** -0.5, 0.25)
    fine_down = normal_values(keys[6], (FFF, C), FFF ** -0.5, 0.125)
    merge_weight = normal_values(keys[7], (4 * C, D2), (4 * C) ** -0.5, 0.125)
    coarse_qkv = draw_coarse_qkv(jax.random.fold_in(keys[14], 71), 0)
    coarse_proj = normal_values(keys[9], (D2, D2), D2 ** -0.5, 0.1875, ((0, 8), (1, 16)))
    coarse_up = normal_values(keys[10], (D2, FFC), D2 ** -0.5, 0.1875, ((0, 16), (1, 8)))
    coarse_down = normal_values(keys[11], (FFC, D2), FFC ** -0.5, 0.09375, ((0, 8), (1, 16)))
    expand_weight = normal_values(keys[12], (D2, 4 * C), D2 ** -0.5, 0.1875)
    out_weight = normal_values(keys[13], (2 * C, C), (2 * C) ** -0.5, 0.1875)
    return dict(fine_tokens=fine_tokens, fine_shift=fine_shift, window_counts=window_counts, fine_qkv=fine_qkv, fine_proj=fine_proj, fine_up=fine_up, fine_down=fine_down, merge_weight=merge_weight, coarse_qkv=coarse_qkv, coarse_proj=coarse_proj, coarse_up=coarse_up, coarse_down=coarse_down, expand_weight=expand_weight, out_weight=out_weight)


def layer_norm(values):
    average = lax.optimization_barrier(jnp.mean(values, axis=-1, keepdims=True))
    centred = values - average
    spread = lax.optimization_barrier(jnp.mean(centred * centred, axis=-1, keepdims=True))
    return centred * lax.rsqrt(spread + 1e-05)

def window_attention(normed, qkv_weight, proj_weight, head_count, head_size, window, counts):
    row_count = normed.shape[0]
    packed = jnp.dot(normed, qkv_weight, preferred_element_type=jnp.float32).astype(jnp.bfloat16)
    packed = lax.optimization_barrier(packed)
    packed = packed.reshape(row_count // window, window, head_count, 3, head_size).astype(jnp.float32)
    queries = packed[:, :, :, 0]
    key_part = packed[:, :, :, 1]
    value_part = packed[:, :, :, 2]
    scores = jnp.einsum('wqhd,wkhd->whqk', queries, key_part) * head_size ** (-0.5)
    if counts is not None:
        position = jnp.arange(window, dtype=jnp.int32)
        visible = position[None, :] < counts[:, None]
        scores = jnp.where(visible[:, None, None, :], scores, -1e+30)
    row_max = lax.optimization_barrier(jnp.max(scores, axis=-1, keepdims=True))
    raised = jnp.exp(scores - row_max)
    weights = (raised / lax.optimization_barrier(jnp.sum(raised, axis=-1, keepdims=True))).astype(jnp.bfloat16)
    weights = lax.optimization_barrier(weights).astype(jnp.float32)
    blended = jnp.einsum('whqk,wkhd->wqhd', weights, value_part).astype(jnp.bfloat16)
    blended = blended.reshape(row_count, head_count * head_size)
    return jnp.dot(blended, proj_weight, preferred_element_type=jnp.float32)

def feed_forward(normed, up_weight, down_weight):
    hidden = jnp.dot(normed, up_weight, preferred_element_type=jnp.float32)
    hidden = jax.nn.gelu(hidden, approximate=False).astype(jnp.bfloat16)
    return jnp.dot(hidden, down_weight, preferred_element_type=jnp.float32)

def reference(fine_tokens, fine_shift, window_counts, fine_qkv, fine_proj, fine_up, fine_down, merge_weight, coarse_qkv, coarse_proj, coarse_up, coarse_down, expand_weight, out_weight):
    offset = fine_shift[0]
    normed = layer_norm(fine_tokens).astype(jnp.bfloat16)
    rolled = jnp.roll(normed, -offset, axis=0)
    attended = window_attention(rolled, fine_qkv, fine_proj, HF, HD, WIN, None)
    fine_mid = fine_tokens + jnp.roll(attended, offset, axis=0)
    fine_out = fine_mid + feed_forward(layer_norm(fine_mid).astype(jnp.bfloat16), fine_up, fine_down)
    merged = fine_out.reshape(fine_out.shape[0] // 4, 4 * fine_out.shape[1])
    grouped = layer_norm(merged).astype(jnp.bfloat16)
    coarse = jnp.dot(grouped, merge_weight, preferred_element_type=jnp.float32)
    coarse_norm = layer_norm(coarse).astype(jnp.bfloat16)
    coarse_mid = coarse + window_attention(coarse_norm, coarse_qkv, coarse_proj, HC, HD, WIN, window_counts)
    coarse_out = coarse_mid + feed_forward(layer_norm(coarse_mid).astype(jnp.bfloat16), coarse_up, coarse_down)
    expanded = jnp.dot(coarse_out.astype(jnp.bfloat16), expand_weight, preferred_element_type=jnp.float32).astype(jnp.bfloat16)
    spread_rows = expanded.reshape(fine_out.shape[0], fine_out.shape[1])
    joined = jnp.concatenate([fine_out.astype(jnp.bfloat16), spread_rows], axis=1)
    return jnp.dot(joined, out_weight, preferred_element_type=jnp.float32)
```

```python
import jax
import jax.numpy as jnp
from jax import lax
from jax.experimental import pallas as pl
from jax.experimental.pallas import tpu as pltpu
from jax.sharding import Mesh, PartitionSpec as P

C = 512
HD = 64
HF = 8
HC = 16
WIN = 144
AXES = ("ylo", "z", "core", "yhi", "x")
STEPS = (0, 1, -1, 2)
F32 = jnp.float32
BF16 = jnp.bfloat16
MIB = 1024 * 1024


def hopped(value, dims, steps):
    pairs = []
    for source in range(128):
        rest, here = source, {}
        for name, size in (("x", 4), ("yhi", 2), ("core", 2), ("z", 4), ("ylo", 2)):
            here[name] = rest % size
            rest //= size
        there = {"x": here["x"], "y": here["yhi"] * 2 + here["ylo"], "z": here["z"]}
        core = here["core"]
        there[dims[core]] = (there[dims[core]] + steps[core]) % 4
        ylo, yhi = there["y"] % 2, there["y"] // 2
        pairs.append((source, (((ylo * 4 + there["z"]) * 2 + core) * 2 + yhi) * 4 + there["x"]))
    return lax.ppermute(value, AXES, pairs)


def direct(value, dims):
    return [value if step == 0 else hopped(value, dims, (step, step)) for step in STEPS]


def core_swap(value):
    return lax.ppermute(value, "core", [(0, 1), (1, 0)])


def normalised(values):
    average = jnp.mean(values, axis=-1, keepdims=True)
    centred = values - average
    spread_of = jnp.mean(centred * centred, axis=-1, keepdims=True)
    return centred * lax.rsqrt(spread_of + 1e-05)


def gelu(hidden):
    return 0.5 * hidden * (1.0 + lax.erf(hidden * (0.5**0.5)))


def dot(a, b):
    return lax.dot_general(a, b, (((1,), (0,)), ((), ())), preferred_element_type=F32)


def dot_t(a, b):
    return lax.dot_general(a, b, (((1,), (1,)), ((), ())), preferred_element_type=F32)


def attend(packed, count):
    queries = packed[:, :HD]
    keys = packed[:, HD : 2 * HD]
    values = packed[:, 2 * HD :]
    scores = dot_t(queries, keys) * HD ** (-0.5)
    if count is not None:
        position = lax.broadcasted_iota(jnp.int32, scores.shape, 1)
        scores = jnp.where(position < count, scores, -1e30)
    row_max = jnp.max(scores, axis=-1, keepdims=True)
    raised = jnp.exp(scores - row_max)
    weights = (raised / jnp.sum(raised, axis=-1, keepdims=True)).astype(BF16)
    return dot(weights, values).astype(BF16)


def vmem(count):
    return [pl.BlockSpec(memory_space=pltpu.VMEM)] * count


def params(mib):
    return pltpu.CompilerParams(vmem_limit_bytes=mib * MIB)


def prepare_kernel(place, tokens, qkv, proj_t, up, down_t, normed, mine, theirs):
    normed[...] = normalised(tokens[...]).astype(BF16)
    halves = [
        (
            jnp.concatenate(
                [qkv[:, 192 * c : 192 * (c + 1)], proj_t[:, HD * c : HD * (c + 1)]], axis=1
            ),
            up[:, 256 * c : 256 * (c + 1)],
            down_t[:, 256 * c : 256 * (c + 1)],
        )
        for c in range(2)
    ]
    for core in range(2):

        @pl.when(place[3] == core)
        def _():
            for unit in range(3):
                mine[unit] = halves[core][unit]
                theirs[unit] = halves[1 - core][unit]


def prepare(place, tokens, qkv, proj_t, up, down_t):
    part = jax.ShapeDtypeStruct((3, 64, 256), BF16)
    return pl.pallas_call(
        prepare_kernel,
        out_shape=(jax.ShapeDtypeStruct(tokens.shape, BF16), part, part),
        in_specs=[pl.BlockSpec(memory_space=pltpu.SMEM)] + vmem(5),
        out_specs=tuple(vmem(3)),
        compiler_params=params(8),
        cost_estimate=pl.CostEstimate(flops=3_000_000, bytes_accessed=2_500_000, transcendentals=0),
        name="prepare",
    )(place, tokens, qkv, proj_t, up, down_t)


def arrange_kernel(kind, place, own, r1, r2, r3, out):
    if kind == "d":
        here = place[2]
    else:
        here = jnp.where(place[3] == 0, place[0], place[1])
    for part, step in zip((own, r1, r2, r3), STEPS):
        at = along(here, -step)
        for unit in range(own.shape[0]):
            out[unit, at] = part[unit]


def arrange(kind, place, parts):
    units = parts[0].shape[0]
    return pl.pallas_call(
        lambda *refs: arrange_kernel(kind, *refs),
        out_shape=jax.ShapeDtypeStruct((units, 4, 128, 256), BF16),
        in_specs=[pl.BlockSpec(memory_space=pltpu.SMEM)] + vmem(4),
        out_specs=pl.BlockSpec(memory_space=pltpu.VMEM),
        compiler_params=params(6),
        cost_estimate=pl.CostEstimate(flops=0, bytes_accessed=1_000_000, transcendentals=0),
        name="arrange_" + kind,
    )(place, *parts)


def along(i, step):
    return lax.rem(i + step + 4, 4)


def fine_attention_kernel(offset, tokens, normed, low, high, qkv, proj, out, ext, packed, blend):
    rows = normed.shape[0]
    shift = offset[0]
    ext[0:WIN, :] = low[...].astype(F32)
    ext[WIN : WIN + rows, :] = normed[...].astype(F32)
    ext[WIN + rows :, :] = high[...].astype(F32)
    rolled = pltpu.roll(ext[...], ext.shape[0] - shift, 0)[: rows + WIN].astype(BF16)
    packed[...] = dot(rolled, qkv[...]).astype(BF16)

    def window(w, carry):
        start = pl.multiple_of(w * WIN, WIN)
        for head in range(HF):
            part = packed[pl.ds(start, WIN), head * 3 * HD : (head + 1) * 3 * HD]
            blend[pl.ds(start, WIN), head * HD : (head + 1) * HD] = attend(part, None)
        return carry

    lax.fori_loop(0, (rows + WIN) // WIN, window, 0)
    ext[0 : rows + WIN, :] = dot(blend[...], proj[...])
    back = pltpu.roll(ext[...], shift + rows + WIN, 0)
    out[...] = tokens[...] + back[:rows]


def fine_attention(offset, tokens, normed, low, high, qkv, proj):
    rows = tokens.shape[0]
    return pl.pallas_call(
        fine_attention_kernel,
        out_shape=jax.ShapeDtypeStruct((rows, C), F32),
        in_specs=[pl.BlockSpec(memory_space=pltpu.SMEM)] + vmem(6),
        out_specs=pl.BlockSpec(memory_space=pltpu.VMEM),
        scratch_shapes=[
            pltpu.VMEM((rows + 2 * WIN, C), F32),
            pltpu.VMEM((rows + WIN, 3 * C), BF16),
            pltpu.VMEM((rows + WIN, C), BF16),
        ],
        compiler_params=params(26),
        cost_estimate=pl.CostEstimate(flops=2_500_000_000, bytes_accessed=6_000_000, transcendentals=900_000),
        name="fine_attention",
    )(offset, tokens, normed, low, high, qkv, proj)


def fine_mlp_kernel(place, counts, mid, up, down, merge, out_weight, skip, coarse, total, lanes):
    rows = mid.shape[0]
    fine = normalised(mid[...]).astype(BF16)
    total[...] = mid[...]
    for part in range(4):
        hidden = gelu(dot(fine, up[:, part * C : (part + 1) * C])).astype(BF16)
        total[...] += dot(hidden, down[part * C : (part + 1) * C, :])
    skip[...] = dot(total[...].astype(BF16), out_weight[:C, :])
    for k in range(4):
        lanes[k] = total[:, k * 128 : (k + 1) * 128]
    pieces = [
        jnp.concatenate([lanes[k, pl.ds(j, rows // 4, stride=4), :] for k in range(4)], axis=1)
        for j in range(4)
    ]
    average = sum(jnp.sum(p, axis=-1, keepdims=True) for p in pieces) * (1.0 / (4 * C))
    pieces = [p - average for p in pieces]
    square = sum(jnp.sum(p * p, axis=-1, keepdims=True) for p in pieces) * (1.0 / (4 * C))
    scale = lax.rsqrt(square + 1e-05)
    result = None
    for j, p in enumerate(pieces):
        term = dot((p * scale).astype(BF16), merge[j * C : (j + 1) * C, :])
        result = term if result is None else result + term
    coarse[:WIN, :] = result
    count = counts[place[1] // 2 * 4 + place[0]]
    coarse[WIN:, :] = jnp.full((8, 2 * C), count, jnp.int32).astype(F32)


def fine_mlp(place, counts, mid, up, down, merge, out_weight):
    rows = mid.shape[0]
    return pl.pallas_call(
        fine_mlp_kernel,
        out_shape=(
            jax.ShapeDtypeStruct((rows, C), F32),
            jax.ShapeDtypeStruct((rows // 4 + 8, 2 * C), F32),
        ),
        in_specs=[pl.BlockSpec(memory_space=pltpu.SMEM)] * 2 + vmem(5),
        out_specs=tuple(vmem(2)),
        scratch_shapes=[pltpu.VMEM((rows, C), F32), pltpu.VMEM((4, rows, 128), F32)],
        compiler_params=params(32),
        cost_estimate=pl.CostEstimate(flops=3_500_000_000, bytes_accessed=12_000_000, transcendentals=1_200_000),
        name="fine_mlp",
    )(place, counts, mid, up, down, merge, out_weight)


def fetch_turned(place, parts, weight, sems):
    x, y, z = place[0], place[1], place[2]
    copies = []
    for at, part in enumerate(parts):
        for slot in range(4):
            sem = sems.at[at * 4 + slot]
            source = part.at[slot]
            from_y, from_z = along(y, -STEPS[slot]), along(z, -STEPS[at])
            zero = pltpu.make_async_copy(
                source, weight.at[lax.div(from_y, 2), :, lax.rem(from_y, 2), from_z], sem
            )
            across_z, across_x = along(z, -STEPS[slot]), along(x, -STEPS[at])
            ones = [
                pltpu.make_async_copy(
                    source.at[pl.ds(2 * yhi, 2)], weight.at[yhi, across_x, :, across_z], sem
                )
                for yhi in range(2)
            ]

            @pl.when(place[3] == 0)
            def _():
                zero.start()

            @pl.when(place[3] == 1)
            def _():
                for one in ones:
                    one.start()

            copies.append(zero)
    return copies


def fetch_down(place, parts, weight, sems):
    x, y = place[0], place[1]
    turn = 1 - 2 * place[3]
    copies = []
    for at, (part, step) in enumerate(zip(parts, (0, -turn, turn, 2))):
        from_y = along(y, step)
        for slot in range(4):
            copy = pltpu.make_async_copy(
                part.at[slot],
                weight.at[lax.div(from_y, 2), along(x, -STEPS[slot]), lax.rem(from_y, 2)],
                sems.at[at * 4 + slot],
            )
            copy.start()
            copies.append(copy)
    return copies


def whole(weight, head):
    return weight[head // 4, head % 4].reshape(2 * C, 256)


def coarse_attention_kernel(place, own, other, a0, a1, a2, a3, out, weight, x, blend, proj, sems):
    copies = fetch_turned(place, (a0, a1, a2, a3), weight, sems)
    x[:WIN, :] = normalised(own[:WIN, :]).astype(BF16)
    x[WIN:, :] = normalised(other[:WIN, :]).astype(BF16)
    counts = [part[WIN : WIN + 1, :1].astype(jnp.int32) for part in (own, other)]
    for copy in copies:
        copy.wait()
    for head in range(8):
        both = whole(weight, head)
        packed = dot(x[...], both[:, : 3 * HD]).astype(BF16)
        for w in range(2):
            blend[w * WIN : (w + 1) * WIN, head * HD : (head + 1) * HD] = attend(
                packed[w * WIN : (w + 1) * WIN], counts[w]
            )
        proj[:, head * HD : (head + 1) * HD] = both[:, 3 * HD :]
    out[...] = dot_t(blend[...], proj[...]).astype(BF16).reshape(out.shape)


def coarse_attention(place, own, other, parts):
    return pl.pallas_call(
        coarse_attention_kernel,
        out_shape=jax.ShapeDtypeStruct((2, WIN, 2 * C), BF16),
        in_specs=[pl.BlockSpec(memory_space=pltpu.SMEM)]
        + vmem(2)
        + [pl.BlockSpec(memory_space=pl.ANY)] * 4,
        out_specs=pl.BlockSpec(memory_space=pltpu.VMEM),
        scratch_shapes=[
            pltpu.VMEM((2, 4, 2, 4, 128, 256), BF16),
            pltpu.VMEM((2 * WIN, 2 * C), BF16),
            pltpu.VMEM((2 * WIN, C), BF16),
            pltpu.VMEM((2 * C, C), BF16),
            pltpu.SemaphoreType.DMA((16,)),
        ],
        compiler_params=params(24),
        cost_estimate=pl.CostEstimate(flops=1_400_000_000, bytes_accessed=7_000_000, transcendentals=400_000),
        name="coarse_attention",
    )(place, own, other, *parts)


def coarse_mlp_kernel(
    place, own, other, sent, came, u0, u1, u2, u3, d0, d1, d2, d3, base, give, up, down, x, hid, sems, late_sems
):
    copies = fetch_turned(place, (u0, u1, u2, u3), up, sems)
    late = fetch_down(place, (d0, d1, d2, d3), down, late_sems)
    mid = own[:WIN, :] + (sent[0].astype(F32) + came[1].astype(F32))
    base[...] = mid
    x[:WIN, :] = normalised(mid).astype(BF16)
    x[WIN:, :] = normalised(other[:WIN, :] + (sent[1].astype(F32) + came[0].astype(F32))).astype(BF16)
    for copy in copies:
        copy.wait()
    for h in range(8):
        hid[h] = gelu(dot(x[...], whole(up, h))).astype(BF16)
    for copy in late:
        copy.wait()
    result = dot_t(hid[0], whole(down, 0))
    for h in range(1, 8):
        result = result + dot_t(hid[h], whole(down, h))
    base[...] += result[:WIN]
    give[...] = result[WIN:].astype(BF16)


def coarse_mlp(place, own, other, sent, came, ups, downs):
    return pl.pallas_call(
        coarse_mlp_kernel,
        out_shape=(
            jax.ShapeDtypeStruct((WIN, 2 * C), F32),
            jax.ShapeDtypeStruct((WIN, 2 * C), BF16),
        ),
        in_specs=[pl.BlockSpec(memory_space=pltpu.SMEM)]
        + vmem(4)
        + [pl.BlockSpec(memory_space=pl.ANY)] * 8,
        out_specs=tuple(vmem(2)),
        scratch_shapes=[
            pltpu.VMEM((2, 4, 2, 4, 128, 256), BF16),
            pltpu.VMEM((2, 4, 2, 4, 128, 256), BF16),
            pltpu.VMEM((2 * WIN, 2 * C), BF16),
            pltpu.VMEM((8, 2 * WIN, 256), BF16),
            pltpu.SemaphoreType.DMA((16,)),
            pltpu.SemaphoreType.DMA((16,)),
        ],
        compiler_params=params(32),
        cost_estimate=pl.CostEstimate(flops=2_400_000_000, bytes_accessed=14_000_000, transcendentals=600_000),
        name="coarse_mlp",
    )(place, own, other, sent, came, *ups, *downs)


def tail_kernel(base, came, skip, expand, out_weight, out, lanes):
    coarse_out = (base[...] + came[...].astype(F32)).astype(BF16)
    for j in range(4):
        rows = dot(coarse_out, expand[:, j * C : (j + 1) * C]).astype(BF16)
        spread_rows = dot(rows, out_weight[C:, :])
        for k in range(4):
            lanes[k, pl.ds(j, WIN, stride=4), :] = spread_rows[:, k * 128 : (k + 1) * 128]
    for k in range(4):
        at = slice(k * 128, (k + 1) * 128)
        out[:, at] = skip[:, at] + lanes[k]


def tail(base, came, skip, expand, out_weight):
    return pl.pallas_call(
        tail_kernel,
        out_shape=jax.ShapeDtypeStruct(skip.shape, F32),
        in_specs=vmem(5),
        out_specs=pl.BlockSpec(memory_space=pltpu.VMEM),
        scratch_shapes=[pltpu.VMEM((4, skip.shape[0], 128), F32)],
        compiler_params=params(20),
        cost_estimate=pl.CostEstimate(flops=900_000_000, bytes_accessed=8_000_000, transcendentals=0),
        name="tail",
    )(base, came, skip, expand, out_weight)


def body(
    fine_tokens,
    fine_shift,
    window_counts,
    fine_qkv,
    fine_proj,
    fine_up,
    fine_down,
    merge_weight,
    coarse_qkv,
    coarse_proj,
    coarse_up,
    coarse_down,
    expand_weight,
    out_weight,
):
    core = lax.axis_index("core")
    y = lax.axis_index("yhi") * 2 + lax.axis_index("ylo")
    place = jnp.stack([lax.axis_index("x"), y, lax.axis_index("z"), core]).astype(jnp.int32)
    normed, mine, theirs = prepare(
        place, fine_tokens, coarse_qkv, coarse_proj.T, coarse_up, coarse_down.T
    )
    got = core_swap(theirs)
    devices = lax.axis_size(AXES)
    up_one = [(i, (i + 1) % devices) for i in range(devices)]
    low = lax.ppermute(normed[-WIN:], AXES, up_one)
    high = lax.ppermute(normed[:WIN], AXES, [(b, a) for a, b in up_one])
    blocks = jnp.where(
        core == 0, jnp.concatenate([mine, got], axis=1), jnp.concatenate([got, mine], axis=1)
    )

    qu = arrange("qu", place, direct(blocks[:2], ("x", "y")))
    d = arrange("d", place, direct(blocks[2:], ("z", "z")))
    qu_two = direct(qu, ("y", "z"))
    d_two = jnp.stack([v[0] for v in direct(d, ("x", "x"))])
    q_two, u_two = (jnp.stack([v[unit] for v in qu_two]) for unit in range(2))
    q_two, u_two, d_two, low, high, normed = lax.optimization_barrier(
        (q_two, u_two, d_two, low, high, normed)
    )
    q_parts = direct(q_two, ("z", "x"))
    d_one = hopped(d_two, ("y", "y"), (1, -1))
    d_other = hopped(d_two, ("y", "y"), (-1, 1))

    mid = fine_attention(fine_shift, fine_tokens, normed, low, high, fine_qkv, fine_proj)
    skip, coarse = fine_mlp(place, window_counts, mid, fine_up, fine_down, merge_weight, out_weight)
    d_one, u_two, coarse = lax.optimization_barrier((d_one, u_two, coarse))
    d_far = hopped(d_one, ("y", "y"), (1, -1))
    u_parts = direct(u_two, ("z", "x"))
    other = core_swap(coarse)
    sent = coarse_attention(place, coarse, other, q_parts)
    came = core_swap(sent)
    base, give = coarse_mlp(
        place, coarse, other, sent, came, u_parts, (d_two, d_one, d_other, d_far)
    )
    return tail(base, core_swap(give), skip, expand_weight, out_weight)


def solution(mesh):
    wide = Mesh(mesh.devices.reshape(2, 4, 2, 2, 4), AXES)
    region, head = ("ylo", "z", "core"), ("yhi", "x")
    in_specs = (
        P(AXES, None),
        P(),
        P(region),
        P(),
        P(),
        P(),
        P(),
        P(),
        P(region, head),
        P(head, region),
        P(region, head),
        P(head, region),
        P(),
        P(),
    )
    return jax.shard_map(body, mesh=wide, in_specs=in_specs, out_specs=P(AXES, None), check_vma=False)
```

```python
import jax
import jax.numpy as jnp
from jax import lax
from jax.experimental import pallas as pl
from jax.experimental.pallas import tpu as pltpu
from jax.sharding import Mesh, PartitionSpec as P

C = 512
HD = 64
HF = 8
HC = 16
WIN = 144
AXES = ("ylo", "z", "core", "yhi", "x")
STEPS = (0, 1, -1, 2)
F32 = jnp.float32
BF16 = jnp.bfloat16
MIB = 1024 * 1024


def hopped(value, dims, steps):
    pairs = []
    for source in range(128):
        rest, here = source, {}
        for name, size in (("x", 4), ("yhi", 2), ("core", 2), ("z", 4), ("ylo", 2)):
            here[name] = rest % size
            rest //= size
        there = {"x": here["x"], "y": here["yhi"] * 2 + here["ylo"], "z": here["z"]}
        core = here["core"]
        there[dims[core]] = (there[dims[core]] + steps[core]) % 4
        ylo, yhi = there["y"] % 2, there["y"] // 2
        pairs.append((source, (((ylo * 4 + there["z"]) * 2 + core) * 2 + yhi) * 4 + there["x"]))
    return lax.ppermute(value, AXES, pairs)


def direct(value, dims):
    return [value if step == 0 else hopped(value, dims, (step, step)) for step in STEPS]


def core_swap(value):
    return lax.ppermute(value, "core", [(0, 1), (1, 0)])


def normalised(values):
    average = jnp.mean(values, axis=-1, keepdims=True)
    centred = values - average
    spread_of = jnp.mean(centred * centred, axis=-1, keepdims=True)
    return centred * lax.rsqrt(spread_of + 1e-05)


def gelu(hidden):
    return 0.5 * hidden * (1.0 + lax.erf(hidden * (0.5**0.5)))


def dot(a, b):
    return lax.dot_general(a, b, (((1,), (0,)), ((), ())), preferred_element_type=F32)


def dot_t(a, b):
    return lax.dot_general(a, b, (((1,), (1,)), ((), ())), preferred_element_type=F32)


def attend(packed, count):
    queries = packed[:, :HD] * jnp.asarray(HD ** (-0.5), BF16)
    keys = packed[:, HD : 2 * HD]
    values = packed[:, 2 * HD :]
    scores = dot_t(queries, keys)
    if count is not None:
        position = lax.broadcasted_iota(jnp.int32, scores.shape, 1)
        scores = jnp.where(position < count, scores, -1e30)
    row_max = jnp.max(scores, axis=-1, keepdims=True)
    raised = jnp.exp(scores - row_max)
    total = jnp.sum(raised, axis=-1, keepdims=True)
    return (dot(raised.astype(BF16), values) * (1.0 / total)).astype(BF16)


def vmem(count):
    return [pl.BlockSpec(memory_space=pltpu.VMEM)] * count


def cost(us):
    return pl.CostEstimate(flops=int(us * 1_150_000_000), bytes_accessed=0, transcendentals=0)


def params(mib):
    return pltpu.CompilerParams(vmem_limit_bytes=mib * MIB)


def norm_kernel(tokens, normed):
    normed[...] = normalised(tokens[...]).astype(BF16)


def norm(tokens):
    return pl.pallas_call(
        norm_kernel,
        out_shape=jax.ShapeDtypeStruct(tokens.shape, BF16),
        in_specs=vmem(1),
        out_specs=pl.BlockSpec(memory_space=pltpu.VMEM),
        compiler_params=params(8),
        cost_estimate=cost(1.0),
        name="norm",
    )(tokens)


def prepare_kernel(place, *refs):
    sources, (mine, theirs), held, sems = refs[:4], refs[4:6], refs[6:10], refs[10]
    copies = [
        pltpu.make_async_copy(source, target, sems.at[i])
        for i, (source, target) in enumerate(zip(sources, held))
    ]
    for copy in copies:
        copy.start()
    for copy in copies:
        copy.wait()
    qkv, proj_t, up, down_t = held
    halves = [
        (
            jnp.concatenate(
                [qkv[:, 192 * c : 192 * (c + 1)], proj_t[:, HD * c : HD * (c + 1)]], axis=1
            ),
            up[:, 256 * c : 256 * (c + 1)],
            down_t[:, 256 * c : 256 * (c + 1)],
        )
        for c in range(2)
    ]
    for core in range(2):

        @pl.when(place[3] == core)
        def _():
            for unit in range(3):
                mine[unit] = halves[core][unit]
                theirs[unit] = halves[1 - core][unit]


def prepare(place, qkv, proj_t, up, down_t):
    part = jax.ShapeDtypeStruct((3, 64, 256), BF16)
    arrays = (qkv, proj_t, up, down_t)
    return pl.pallas_call(
        prepare_kernel,
        out_shape=(part, part),
        in_specs=[pl.BlockSpec(memory_space=pltpu.SMEM)]
        + [pl.BlockSpec(memory_space=pltpu.HBM)] * 4,
        out_specs=tuple(vmem(2)),
        scratch_shapes=[pltpu.VMEM(v.shape, v.dtype) for v in arrays]
        + [pltpu.SemaphoreType.DMA((4,))],
        compiler_params=params(60),
        cost_estimate=cost(1.5),
        name="prepare",
    )(place, *arrays)


def arrange_kernel(place, own, r1, r2, r3, turned, down):
    here = jnp.where(place[3] == 0, place[0], place[2])
    for part, step in zip((own, r1, r2, r3), STEPS):
        at = along(here, -step)
        turned[0, at] = part[0]
        turned[1, at] = part[1]
        down[at] = part[2]


def arrange(place, parts):
    return pl.pallas_call(
        arrange_kernel,
        out_shape=(
            jax.ShapeDtypeStruct((2, 4, 128, 256), BF16),
            jax.ShapeDtypeStruct((4, 128, 256), BF16),
        ),
        in_specs=[pl.BlockSpec(memory_space=pltpu.SMEM)] + vmem(4),
        out_specs=tuple(vmem(2)),
        compiler_params=params(6),
        cost_estimate=cost(0.7),
        name="arrange",
    )(place, *parts)


def along(i, step):
    return lax.rem(i + step + 4, 4)


def fine_attention_kernel(offset, tokens, normed, low, high, qkv, proj, out, ext, packed, blend):
    rows = normed.shape[0]
    shift = offset[0]
    ext[0:WIN, :] = low[...].astype(F32)
    ext[WIN : WIN + rows, :] = normed[...].astype(F32)
    ext[WIN + rows :, :] = high[...].astype(F32)
    rolled = pltpu.roll(ext[...], ext.shape[0] - shift, 0)[: rows + WIN].astype(BF16)
    packed[...] = dot(rolled, qkv[...]).astype(BF16)

    def window(w, carry):
        start = pl.multiple_of(w * WIN, WIN)
        for head in range(HF):
            part = packed[pl.ds(start, WIN), head * 3 * HD : (head + 1) * 3 * HD]
            blend[pl.ds(start, WIN), head * HD : (head + 1) * HD] = attend(part, None)
        return carry

    lax.fori_loop(0, (rows + WIN) // WIN, window, 0)
    ext[0 : rows + WIN, :] = dot(blend[...], proj[...])
    back = pltpu.roll(ext[...], shift + rows + WIN, 0)
    out[...] = tokens[...] + back[:rows]


def fine_attention(offset, tokens, normed, low, high, qkv, proj):
    rows = tokens.shape[0]
    return pl.pallas_call(
        fine_attention_kernel,
        out_shape=jax.ShapeDtypeStruct((rows, C), F32),
        in_specs=[pl.BlockSpec(memory_space=pltpu.SMEM)] + vmem(6),
        out_specs=pl.BlockSpec(memory_space=pltpu.VMEM),
        scratch_shapes=[
            pltpu.VMEM((rows + 2 * WIN, C), F32),
            pltpu.VMEM((rows + WIN, 3 * C), BF16),
            pltpu.VMEM((rows + WIN, C), BF16),
        ],
        compiler_params=params(26),
        cost_estimate=pl.CostEstimate(flops=2_500_000_000, bytes_accessed=6_000_000, transcendentals=900_000),
        name="fine_attention",
    )(offset, tokens, normed, low, high, qkv, proj)


def fine_mlp_kernel(place, counts, mid, up, down, merge, out_weight, skip, coarse, total, lanes):
    rows = mid.shape[0]
    fine = normalised(mid[...]).astype(BF16)
    total[...] = mid[...]
    for part in range(4):
        hidden = gelu(dot(fine, up[:, part * C : (part + 1) * C])).astype(BF16)
        total[...] += dot(hidden, down[part * C : (part + 1) * C, :])
    skip[...] = dot(total[...].astype(BF16), out_weight[:C, :])
    for k in range(4):
        lanes[k] = total[:, k * 128 : (k + 1) * 128]
    pieces = [
        jnp.concatenate([lanes[k, pl.ds(j, rows // 4, stride=4), :] for k in range(4)], axis=1)
        for j in range(4)
    ]
    average = sum(jnp.sum(p, axis=-1, keepdims=True) for p in pieces) * (1.0 / (4 * C))
    pieces = [p - average for p in pieces]
    square = sum(jnp.sum(p * p, axis=-1, keepdims=True) for p in pieces) * (1.0 / (4 * C))
    scale = lax.rsqrt(square + 1e-05)
    result = None
    for j, p in enumerate(pieces):
        term = dot((p * scale).astype(BF16), merge[j * C : (j + 1) * C, :])
        result = term if result is None else result + term
    coarse[:WIN, :] = result
    count = counts[place[1] // 2 * 4 + place[0]]
    coarse[WIN:, :] = jnp.full((8, 2 * C), count, jnp.int32).astype(F32)


def fine_mlp(place, counts, mid, up, down, merge, out_weight):
    rows = mid.shape[0]
    return pl.pallas_call(
        fine_mlp_kernel,
        out_shape=(
            jax.ShapeDtypeStruct((rows, C), F32),
            jax.ShapeDtypeStruct((rows // 4 + 8, 2 * C), F32),
        ),
        in_specs=[pl.BlockSpec(memory_space=pltpu.SMEM)] * 2 + vmem(5),
        out_specs=tuple(vmem(2)),
        scratch_shapes=[pltpu.VMEM((rows, C), F32), pltpu.VMEM((4, rows, 128), F32)],
        compiler_params=params(32),
        cost_estimate=pl.CostEstimate(flops=3_500_000_000, bytes_accessed=12_000_000, transcendentals=1_200_000),
        name="fine_mlp",
    )(place, counts, mid, up, down, merge, out_weight)


def fetch(place, pieces, weight, sems):
    copies = []
    for at, (source, y, z, x) in enumerate(pieces):
        yhi, ylo = lax.div(y, 2), lax.rem(y, 2)
        zero = pltpu.make_async_copy(source, weight.at[yhi, :, ylo, z], sems.at[at])
        one = pltpu.make_async_copy(source, weight.at[yhi, x, ylo], sems.at[at])

        @pl.when(place[3] == 0)
        def _():
            zero.start()

        @pl.when(place[3] == 1)
        def _():
            one.start()

        copies.append(zero)
    return copies


def fetch_turned(place, parts, weight, sems):
    x, y, z = place[0], place[1], place[2]
    turn = 1 - 2 * place[3]
    return fetch(
        place,
        [
            (parts[at].at[slot], along(y, step), along(z, -STEPS[at]), along(x, -STEPS[at]))
            for at in range(4)
            for slot, step in enumerate((0, -turn, turn, 2))
        ],
        weight,
        sems,
    )


def fetch_down(place, parts, weight, sems):
    x, y, z = place[0], place[1], place[2]
    turn = 1 - 2 * place[3]
    return fetch(
        place,
        [
            (part.at[slot], along(y, step), along(z, -STEPS[slot]), along(x, -STEPS[slot]))
            for part, step in zip(parts, (0, -turn, turn, 2))
            for slot in range(4)
        ],
        weight,
        sems,
    )


def whole(weight, head):
    return weight[head // 4, head % 4].reshape(2 * C, 256)


def coarse_attention_kernel(place, own, other, a0, a1, a2, a3, out, weight, x, blend, proj, sems):
    copies = fetch_turned(place, (a0, a1, a2, a3), weight, sems)
    x[:WIN, :] = normalised(own[:WIN, :]).astype(BF16)
    x[WIN:, :] = normalised(other[:WIN, :]).astype(BF16)
    counts = [part[WIN : WIN + 1, :1].astype(jnp.int32) for part in (own, other)]
    for copy in copies:
        copy.wait()
    for head in range(8):
        both = whole(weight, head)
        packed = dot(x[...], both[:, : 3 * HD]).astype(BF16)
        for w in range(2):
            blend[w * WIN : (w + 1) * WIN, head * HD : (head + 1) * HD] = attend(
                packed[w * WIN : (w + 1) * WIN], counts[w]
            )
        proj[:, head * HD : (head + 1) * HD] = both[:, 3 * HD :]
    out[...] = dot_t(blend[...], proj[...]).astype(BF16).reshape(out.shape)


def coarse_attention(place, own, other, parts):
    return pl.pallas_call(
        coarse_attention_kernel,
        out_shape=jax.ShapeDtypeStruct((2, WIN, 2 * C), BF16),
        in_specs=[pl.BlockSpec(memory_space=pltpu.SMEM)]
        + vmem(2)
        + [pl.BlockSpec(memory_space=pl.ANY)] * 4,
        out_specs=pl.BlockSpec(memory_space=pltpu.VMEM),
        scratch_shapes=[
            pltpu.VMEM((2, 4, 2, 4, 128, 256), BF16),
            pltpu.VMEM((2 * WIN, 2 * C), BF16),
            pltpu.VMEM((2 * WIN, C), BF16),
            pltpu.VMEM((2 * C, C), BF16),
            pltpu.SemaphoreType.DMA((16,)),
        ],
        compiler_params=params(24),
        cost_estimate=pl.CostEstimate(flops=1_400_000_000, bytes_accessed=7_000_000, transcendentals=400_000),
        name="coarse_attention",
    )(place, own, other, *parts)


def coarse_mlp_kernel(
    place, own, other, sent, came, u0, u1, u2, u3, d0, d1, d2, d3, base, give, up, down, x, hid, sems, late_sems
):
    copies = fetch_turned(place, (u0, u1, u2, u3), up, sems)
    late = fetch_down(place, (d0, d1, d2, d3), down, late_sems)
    mid = own[:WIN, :] + (sent[0].astype(F32) + came[1].astype(F32))
    base[...] = mid
    x[:WIN, :] = normalised(mid).astype(BF16)
    x[WIN:, :] = normalised(other[:WIN, :] + (sent[1].astype(F32) + came[0].astype(F32))).astype(BF16)
    for copy in copies:
        copy.wait()
    for h in range(8):
        hid[h] = gelu(dot(x[...], whole(up, h))).astype(BF16)
    for copy in late:
        copy.wait()
    result = dot_t(hid[0], whole(down, 0))
    for h in range(1, 8):
        result = result + dot_t(hid[h], whole(down, h))
    base[...] += result[:WIN]
    give[...] = result[WIN:].astype(BF16)


def coarse_mlp(place, own, other, sent, came, ups, downs):
    return pl.pallas_call(
        coarse_mlp_kernel,
        out_shape=(
            jax.ShapeDtypeStruct((WIN, 2 * C), F32),
            jax.ShapeDtypeStruct((WIN, 2 * C), BF16),
        ),
        in_specs=[pl.BlockSpec(memory_space=pltpu.SMEM)]
        + vmem(4)
        + [pl.BlockSpec(memory_space=pl.ANY)] * 8,
        out_specs=tuple(vmem(2)),
        scratch_shapes=[
            pltpu.VMEM((2, 4, 2, 4, 128, 256), BF16),
            pltpu.VMEM((2, 4, 2, 4, 128, 256), BF16),
            pltpu.VMEM((2 * WIN, 2 * C), BF16),
            pltpu.VMEM((8, 2 * WIN, 256), BF16),
            pltpu.SemaphoreType.DMA((16,)),
            pltpu.SemaphoreType.DMA((16,)),
        ],
        compiler_params=params(32),
        cost_estimate=pl.CostEstimate(flops=2_400_000_000, bytes_accessed=14_000_000, transcendentals=600_000),
        name="coarse_mlp",
    )(place, own, other, sent, came, *ups, *downs)


def tail_kernel(base, came, skip, expand, out_weight, out, lanes):
    coarse_out = (base[...] + came[...].astype(F32)).astype(BF16)
    for j in range(4):
        rows = dot(coarse_out, expand[:, j * C : (j + 1) * C]).astype(BF16)
        spread_rows = dot(rows, out_weight[C:, :])
        for k in range(4):
            lanes[k, pl.ds(j, WIN, stride=4), :] = spread_rows[:, k * 128 : (k + 1) * 128]
    for k in range(4):
        at = slice(k * 128, (k + 1) * 128)
        out[:, at] = skip[:, at] + lanes[k]


def tail(base, came, skip, expand, out_weight):
    return pl.pallas_call(
        tail_kernel,
        out_shape=jax.ShapeDtypeStruct(skip.shape, F32),
        in_specs=vmem(5),
        out_specs=pl.BlockSpec(memory_space=pltpu.VMEM),
        scratch_shapes=[pltpu.VMEM((4, skip.shape[0], 128), F32)],
        compiler_params=params(20),
        cost_estimate=pl.CostEstimate(flops=900_000_000, bytes_accessed=8_000_000, transcendentals=0),
        name="tail",
    )(base, came, skip, expand, out_weight)


def body(
    fine_tokens,
    fine_shift,
    window_counts,
    fine_qkv,
    fine_proj,
    fine_up,
    fine_down,
    merge_weight,
    coarse_qkv,
    coarse_proj,
    coarse_up,
    coarse_down,
    expand_weight,
    out_weight,
):
    core = lax.axis_index("core")
    y = lax.axis_index("yhi") * 2 + lax.axis_index("ylo")
    place = jnp.stack([lax.axis_index("x"), y, lax.axis_index("z"), core]).astype(jnp.int32)
    mine, theirs = prepare(place, coarse_qkv, coarse_proj.T, coarse_up, coarse_down.T)
    tokens, theirs = lax.optimization_barrier((fine_tokens, theirs))
    normed = norm(tokens)
    got = core_swap(theirs)
    devices = lax.axis_size(AXES)
    up_one = [(i, (i + 1) % devices) for i in range(devices)]
    low = lax.ppermute(normed[-WIN:], AXES, up_one)
    high = lax.ppermute(normed[:WIN], AXES, [(b, a) for a, b in up_one])
    blocks = jnp.where(
        core == 0, jnp.concatenate([mine, got], axis=1), jnp.concatenate([got, mine], axis=1)
    )

    qu, d = arrange(place, direct(blocks, ("x", "z")))
    qu_one, qu_other = (hopped(qu, ("y", "y"), (step, -step)) for step in (1, -1))
    d_near = [d] + [hopped(d, ("z", "x"), (step, step)) for step in (1, -1)]

    qu, low, high, normed = lax.optimization_barrier((qu, low, high, normed))
    mid = fine_attention(fine_shift, fine_tokens, normed, low, high, fine_qkv, fine_proj)

    qu_one, qu_other, d_near, mid = lax.optimization_barrier((qu_one, qu_other, d_near, mid))
    qu_far = hopped(qu_one, ("y", "y"), (1, -1))
    d_far = hopped(d_near[0], ("z", "x"), (2, 2))
    skip, coarse = fine_mlp(place, window_counts, mid, fine_up, fine_down, merge_weight, out_weight)

    qu_far, d_far, coarse = lax.optimization_barrier((qu_far, d_far, coarse))
    q_two, u_two = (jnp.stack([v[i] for v in (qu, qu_one, qu_other, qu_far)]) for i in range(2))
    d_two = jnp.stack([*d_near, d_far])
    q_one, q_other, q_far = (hopped(q_two, ("z", "x"), (step, step)) for step in (1, -1, 2))
    d_one, d_other = (hopped(d_two, ("y", "y"), (step, -step)) for step in (1, -1))
    other = core_swap(coarse)
    q_other, u_two = lax.optimization_barrier((q_other, u_two))
    u_parts = direct(u_two, ("z", "x"))
    d_far = hopped(d_one, ("y", "y"), (1, -1))
    sent = coarse_attention(place, coarse, other, (q_two, q_one, q_other, q_far))
    came = core_swap(sent)
    base, give = coarse_mlp(
        place, coarse, other, sent, came, u_parts, (d_two, d_one, d_other, d_far)
    )
    return tail(base, core_swap(give), skip, expand_weight, out_weight)


def solution(mesh):
    wide = Mesh(mesh.devices.reshape(2, 4, 2, 2, 4), AXES)
    region, head = ("ylo", "z", "core"), ("yhi", "x")
    in_specs = (
        P(AXES, None),
        P(),
        P(region),
        P(),
        P(),
        P(),
        P(),
        P(),
        P(region, head),
        P(head, region),
        P(region, head),
        P(head, region),
        P(),
        P(),
    )
    return jax.shard_map(body, mesh=wide, in_specs=in_specs, out_specs=P(AXES, None), check_vma=False)
```

```python
import jax
import jax.numpy as jnp
from jax import lax
from jax.experimental import pallas as pl
from jax.experimental.pallas import tpu as pltpu
from jax.sharding import Mesh, PartitionSpec as P

C = 512
HD = 64
HF = 8
HC = 16
WIN = 144
AXES = ("ylo", "z", "core", "yhi", "x")
STEPS = (0, 1, -1, 2)
F32 = jnp.float32
BF16 = jnp.bfloat16
MIB = 1024 * 1024


def hopped(value, dims, steps):
    pairs = []
    for source in range(128):
        rest, here = source, {}
        for name, size in (("x", 4), ("yhi", 2), ("core", 2), ("z", 4), ("ylo", 2)):
            here[name] = rest % size
            rest //= size
        there = {"x": here["x"], "y": here["yhi"] * 2 + here["ylo"], "z": here["z"]}
        core = here["core"]
        there[dims[core]] = (there[dims[core]] + steps[core]) % 4
        ylo, yhi = there["y"] % 2, there["y"] // 2
        pairs.append((source, (((ylo * 4 + there["z"]) * 2 + core) * 2 + yhi) * 4 + there["x"]))
    return lax.ppermute(value, AXES, pairs)


def direct(value, dims):
    return [value if step == 0 else hopped(value, dims, (step, step)) for step in STEPS]


def core_swap(value):
    return lax.ppermute(value, "core", [(0, 1), (1, 0)])


def normalised(values):
    average = jnp.mean(values, axis=-1, keepdims=True)
    centred = values - average
    spread_of = jnp.mean(centred * centred, axis=-1, keepdims=True)
    return centred * lax.rsqrt(spread_of + 1e-05)


def gelu(hidden):
    return 0.5 * hidden * (1.0 + lax.erf(hidden * (0.5**0.5)))


def dot(a, b):
    return lax.dot_general(a, b, (((1,), (0,)), ((), ())), preferred_element_type=F32)


def dot_t(a, b):
    return lax.dot_general(a, b, (((1,), (1,)), ((), ())), preferred_element_type=F32)


def attend(packed, count):
    queries = packed[:, :HD] * jnp.asarray(HD ** (-0.5), BF16)
    keys = packed[:, HD : 2 * HD]
    values = packed[:, 2 * HD :]
    scores = dot_t(queries, keys)
    if count is not None:
        position = lax.broadcasted_iota(jnp.int32, scores.shape, 1)
        scores = jnp.where(position < count, scores, -1e30)
    row_max = jnp.max(scores, axis=-1, keepdims=True)
    raised = jnp.exp(scores - row_max)
    total = jnp.sum(raised, axis=-1, keepdims=True)
    return (dot(raised.astype(BF16), values) * (1.0 / total)).astype(BF16)


def vmem(count):
    return [pl.BlockSpec(memory_space=pltpu.VMEM)] * count


def cost(us):
    return pl.CostEstimate(flops=int(us * 1_150_000_000), bytes_accessed=0, transcendentals=0)


def params(mib):
    return pltpu.CompilerParams(vmem_limit_bytes=mib * MIB)


def norm_kernel(tokens, normed):
    normed[...] = normalised(tokens[...]).astype(BF16)


def norm(tokens):
    return pl.pallas_call(
        norm_kernel,
        out_shape=jax.ShapeDtypeStruct(tokens.shape, BF16),
        in_specs=vmem(1),
        out_specs=pl.BlockSpec(memory_space=pltpu.VMEM),
        compiler_params=params(8),
        cost_estimate=cost(1.0),
        name="norm",
    )(tokens)


def prepare_kernel(place, *refs):
    sources, (mine, theirs), held, sems = refs[:4], refs[4:6], refs[6:10], refs[10]
    copies = [
        pltpu.make_async_copy(source, target, sems.at[i])
        for i, (source, target) in enumerate(zip(sources, held))
    ]
    for copy in copies:
        copy.start()
    for copy in copies:
        copy.wait()
    qkv, proj_t, up, down_t = held
    halves = [
        (
            jnp.concatenate(
                [qkv[:, 192 * c : 192 * (c + 1)], proj_t[:, HD * c : HD * (c + 1)]], axis=1
            ),
            up[:, 256 * c : 256 * (c + 1)],
            down_t[:, 256 * c : 256 * (c + 1)],
        )
        for c in range(2)
    ]
    for core in range(2):

        @pl.when(place[3] == core)
        def _():
            for unit in range(3):
                mine[unit] = halves[core][unit]
                theirs[unit] = halves[1 - core][unit]


def prepare(place, qkv, proj_t, up, down_t):
    part = jax.ShapeDtypeStruct((3, 64, 256), BF16)
    arrays = (qkv, proj_t, up, down_t)
    return pl.pallas_call(
        prepare_kernel,
        out_shape=(part, part),
        in_specs=[pl.BlockSpec(memory_space=pltpu.SMEM)]
        + [pl.BlockSpec(memory_space=pltpu.HBM)] * 4,
        out_specs=tuple(vmem(2)),
        scratch_shapes=[pltpu.VMEM(v.shape, v.dtype) for v in arrays]
        + [pltpu.SemaphoreType.DMA((4,))],
        compiler_params=params(60),
        cost_estimate=cost(1.5),
        name="prepare",
    )(place, *arrays)


UP = 96


def arrange_kernel(place, own, r1, r2, r3, turned, down):
    here = jnp.where(place[3] == 0, place[0], place[2])
    for part, step in zip((own, r1, r2, r3), STEPS):
        at = along(here, -step)
        turned[at, :128] = part[0]
        turned[at, 128:] = part[1, :UP]
        down[at, :128] = part[2]
        down[at, 128:] = part[1, UP:]


def arrange(place, parts):
    return pl.pallas_call(
        arrange_kernel,
        out_shape=(
            jax.ShapeDtypeStruct((4, 128 + UP, 256), BF16),
            jax.ShapeDtypeStruct((4, 256 - UP, 256), BF16),
        ),
        in_specs=[pl.BlockSpec(memory_space=pltpu.SMEM)] + vmem(4),
        out_specs=tuple(vmem(2)),
        compiler_params=params(6),
        cost_estimate=cost(0.7),
        name="arrange",
    )(place, *parts)


def along(i, step):
    return lax.rem(i + step + 4, 4)


def fine_attention_kernel(offset, tokens, normed, low, high, qkv, proj, out, ext, packed, blend):
    rows = normed.shape[0]
    shift = offset[0]
    ext[0:WIN, :] = low[...].astype(F32)
    ext[WIN : WIN + rows, :] = normed[...].astype(F32)
    ext[WIN + rows :, :] = high[...].astype(F32)
    rolled = pltpu.roll(ext[...], ext.shape[0] - shift, 0)[: rows + WIN].astype(BF16)
    packed[...] = dot(rolled, qkv[...]).astype(BF16)

    def window(w, carry):
        start = pl.multiple_of(w * WIN, WIN)
        for head in range(HF):
            part = packed[pl.ds(start, WIN), head * 3 * HD : (head + 1) * 3 * HD]
            blend[pl.ds(start, WIN), head * HD : (head + 1) * HD] = attend(part, None)
        return carry

    lax.fori_loop(0, (rows + WIN) // WIN, window, 0)
    ext[0 : rows + WIN, :] = dot(blend[...], proj[...])
    back = pltpu.roll(ext[...], shift + rows + WIN, 0)
    out[...] = tokens[...] + back[:rows]


def fine_attention(offset, tokens, normed, low, high, qkv, proj):
    rows = tokens.shape[0]
    return pl.pallas_call(
        fine_attention_kernel,
        out_shape=jax.ShapeDtypeStruct((rows, C), F32),
        in_specs=[pl.BlockSpec(memory_space=pltpu.SMEM)] + vmem(6),
        out_specs=pl.BlockSpec(memory_space=pltpu.VMEM),
        scratch_shapes=[
            pltpu.VMEM((rows + 2 * WIN, C), F32),
            pltpu.VMEM((rows + WIN, 3 * C), BF16),
            pltpu.VMEM((rows + WIN, C), BF16),
        ],
        compiler_params=params(26),
        cost_estimate=pl.CostEstimate(flops=2_500_000_000, bytes_accessed=6_000_000, transcendentals=900_000),
        name="fine_attention",
    )(offset, tokens, normed, low, high, qkv, proj)


def fine_mlp_kernel(place, counts, mid, up, down, merge, out_weight, skip, coarse, total, lanes):
    rows = mid.shape[0]
    fine = normalised(mid[...]).astype(BF16)
    total[...] = mid[...]
    for part in range(4):
        hidden = gelu(dot(fine, up[:, part * C : (part + 1) * C])).astype(BF16)
        total[...] += dot(hidden, down[part * C : (part + 1) * C, :])
    skip[...] = dot(total[...].astype(BF16), out_weight[:C, :])
    for k in range(4):
        lanes[k] = total[:, k * 128 : (k + 1) * 128]
    pieces = [
        jnp.concatenate([lanes[k, pl.ds(j, rows // 4, stride=4), :] for k in range(4)], axis=1)
        for j in range(4)
    ]
    average = sum(jnp.sum(p, axis=-1, keepdims=True) for p in pieces) * (1.0 / (4 * C))
    pieces = [p - average for p in pieces]
    square = sum(jnp.sum(p * p, axis=-1, keepdims=True) for p in pieces) * (1.0 / (4 * C))
    scale = lax.rsqrt(square + 1e-05)
    result = None
    for j, p in enumerate(pieces):
        term = dot((p * scale).astype(BF16), merge[j * C : (j + 1) * C, :])
        result = term if result is None else result + term
    coarse[:WIN, :] = result
    count = counts[place[1] // 2 * 4 + place[0]]
    coarse[WIN:, :] = jnp.full((8, 2 * C), count, jnp.int32).astype(F32)


def fine_mlp(place, counts, mid, up, down, merge, out_weight):
    rows = mid.shape[0]
    return pl.pallas_call(
        fine_mlp_kernel,
        out_shape=(
            jax.ShapeDtypeStruct((rows, C), F32),
            jax.ShapeDtypeStruct((rows // 4 + 8, 2 * C), F32),
        ),
        in_specs=[pl.BlockSpec(memory_space=pltpu.SMEM)] * 2 + vmem(5),
        out_specs=tuple(vmem(2)),
        scratch_shapes=[pltpu.VMEM((rows, C), F32), pltpu.VMEM((4, rows, 128), F32)],
        compiler_params=params(32),
        cost_estimate=pl.CostEstimate(flops=3_500_000_000, bytes_accessed=12_000_000, transcendentals=1_200_000),
        name="fine_mlp",
    )(place, counts, mid, up, down, merge, out_weight)


def fetch(place, pieces, weight, sems, first=0):
    zeros, ones = [], []
    for at, (source, y, z, x) in enumerate(pieces):
        yhi, ylo = lax.div(y, 2), lax.rem(y, 2)
        rows = pl.ds(first, source.shape[1])
        zeros.append(
            pltpu.make_async_copy(source, weight.at[yhi, :, ylo, z, rows], sems.at[at])
        )
        ones.append(
            pltpu.make_async_copy(source, weight.at[yhi, x, ylo, :, rows], sems.at[at])
        )

    @pl.when(place[3] == 0)
    def _():
        for copy in zeros:
            copy.start()

    @pl.when(place[3] == 1)
    def _():
        for copy in ones:
            copy.start()

    return zeros


def fetch_turned(place, parts, weight, sems):
    x, y, z = place[0], place[1], place[2]
    turn = 1 - 2 * place[3]
    return fetch(
        place,
        [
            (parts[at].at[slot], along(y, step), along(z, -STEPS[at]), along(x, -STEPS[at]))
            for at in range(4)
            for slot, step in enumerate((0, -turn, turn, 2))
        ],
        weight,
        sems,
    )


def fetch_down(place, parts, rows, weight, sems, first=0):
    x, y, z = place[0], place[1], place[2]
    turn = 1 - 2 * place[3]
    return fetch(
        place,
        [
            (part.at[slot, :, rows], along(y, step), along(z, -STEPS[slot]), along(x, -STEPS[slot]))
            for part, step in zip(parts, (0, -turn, turn, 2))
            for slot in range(4)
        ],
        weight,
        sems,
        first,
    )


def whole(weight, head):
    return weight[head // 4, head % 4].reshape(2 * C, 256)


def coarse_attention_kernel(place, own, other, a0, a1, a2, a3, out, weight, x, blend, proj, sems):
    copies = fetch_turned(place, (a0, a1, a2, a3), weight, sems)
    x[:WIN, :] = normalised(own[:WIN, :]).astype(BF16)
    x[WIN:, :] = normalised(other[:WIN, :]).astype(BF16)
    counts = [part[WIN : WIN + 1, :1].astype(jnp.int32) for part in (own, other)]
    for copy in copies:
        copy.wait()
    for head in range(8):
        both = whole(weight, head)
        packed = dot(x[...], both[:, : 3 * HD]).astype(BF16)
        for w in range(2):
            blend[w * WIN : (w + 1) * WIN, head * HD : (head + 1) * HD] = attend(
                packed[w * WIN : (w + 1) * WIN], counts[w]
            )
        proj[:, head * HD : (head + 1) * HD] = both[:, 3 * HD :]
    out[...] = dot_t(blend[...], proj[...]).astype(BF16).reshape(out.shape)


def coarse_attention(place, own, other, parts):
    return pl.pallas_call(
        coarse_attention_kernel,
        out_shape=jax.ShapeDtypeStruct((2, WIN, 2 * C), BF16),
        in_specs=[pl.BlockSpec(memory_space=pltpu.SMEM)]
        + vmem(2)
        + [pl.BlockSpec(memory_space=pl.ANY)] * 4,
        out_specs=pl.BlockSpec(memory_space=pltpu.VMEM),
        scratch_shapes=[
            pltpu.VMEM((2, 4, 2, 4, 128, 256), BF16),
            pltpu.VMEM((2 * WIN, 2 * C), BF16),
            pltpu.VMEM((2 * WIN, C), BF16),
            pltpu.VMEM((2 * C, C), BF16),
            pltpu.SemaphoreType.DMA((16,)),
        ],
        compiler_params=params(24),
        cost_estimate=pl.CostEstimate(flops=1_400_000_000, bytes_accessed=7_000_000, transcendentals=400_000),
        name="coarse_attention",
    )(place, own, other, *parts)


def coarse_mlp_kernel(
    place, own, other, sent, came, u0, u1, u2, u3, d0, d1, d2, d3, base, give, up, down, x, hid, sems, rest_sems, late_sems
):
    copies = fetch_turned(place, (u0, u1, u2, u3), up, sems)
    downs = (d0, d1, d2, d3)
    copies += fetch_down(place, downs, pl.ds(128, 128 - UP), up, rest_sems, UP)
    mid = own[:WIN, :] + (sent[0].astype(F32) + came[1].astype(F32))
    base[...] = mid
    x[:WIN, :] = normalised(mid).astype(BF16)
    x[WIN:, :] = normalised(other[:WIN, :] + (sent[1].astype(F32) + came[0].astype(F32))).astype(BF16)
    late = fetch_down(place, downs, pl.ds(0, 128), down, late_sems)
    for copy in copies:
        copy.wait()
    for h in range(8):
        hid[h] = gelu(dot(x[...], whole(up, h))).astype(BF16)
    for copy in late:
        copy.wait()
    result = dot_t(hid[0], whole(down, 0))
    for h in range(1, 8):
        result = result + dot_t(hid[h], whole(down, h))
    base[...] += result[:WIN]
    give[...] = result[WIN:].astype(BF16)


def coarse_mlp(place, own, other, sent, came, ups, downs):
    return pl.pallas_call(
        coarse_mlp_kernel,
        out_shape=(
            jax.ShapeDtypeStruct((WIN, 2 * C), F32),
            jax.ShapeDtypeStruct((WIN, 2 * C), BF16),
        ),
        in_specs=[pl.BlockSpec(memory_space=pltpu.SMEM)]
        + vmem(4)
        + [pl.BlockSpec(memory_space=pl.ANY)] * 8,
        out_specs=tuple(vmem(2)),
        scratch_shapes=[
            pltpu.VMEM((2, 4, 2, 4, 128, 256), BF16),
            pltpu.VMEM((2, 4, 2, 4, 128, 256), BF16),
            pltpu.VMEM((2 * WIN, 2 * C), BF16),
            pltpu.VMEM((8, 2 * WIN, 256), BF16),
            pltpu.SemaphoreType.DMA((16,)),
            pltpu.SemaphoreType.DMA((16,)),
            pltpu.SemaphoreType.DMA((16,)),
        ],
        compiler_params=params(32),
        cost_estimate=pl.CostEstimate(flops=2_400_000_000, bytes_accessed=14_000_000, transcendentals=600_000),
        name="coarse_mlp",
    )(place, own, other, sent, came, *ups, *downs)


def tail_kernel(base, came, skip, expand, out_weight, out, lanes):
    coarse_out = (base[...] + came[...].astype(F32)).astype(BF16)
    for j in range(4):
        rows = dot(coarse_out, expand[:, j * C : (j + 1) * C]).astype(BF16)
        spread_rows = dot(rows, out_weight[C:, :])
        for k in range(4):
            lanes[k, pl.ds(j, WIN, stride=4), :] = spread_rows[:, k * 128 : (k + 1) * 128]
    for k in range(4):
        at = slice(k * 128, (k + 1) * 128)
        out[:, at] = skip[:, at] + lanes[k]


def tail(base, came, skip, expand, out_weight):
    return pl.pallas_call(
        tail_kernel,
        out_shape=jax.ShapeDtypeStruct(skip.shape, F32),
        in_specs=vmem(5),
        out_specs=pl.BlockSpec(memory_space=pltpu.VMEM),
        scratch_shapes=[pltpu.VMEM((4, skip.shape[0], 128), F32)],
        compiler_params=params(20),
        cost_estimate=pl.CostEstimate(flops=900_000_000, bytes_accessed=8_000_000, transcendentals=0),
        name="tail",
    )(base, came, skip, expand, out_weight)


def body(
    fine_tokens,
    fine_shift,
    window_counts,
    fine_qkv,
    fine_proj,
    fine_up,
    fine_down,
    merge_weight,
    coarse_qkv,
    coarse_proj,
    coarse_up,
    coarse_down,
    expand_weight,
    out_weight,
):
    core = lax.axis_index("core")
    y = lax.axis_index("yhi") * 2 + lax.axis_index("ylo")
    place = jnp.stack([lax.axis_index("x"), y, lax.axis_index("z"), core]).astype(jnp.int32)
    mine, theirs = prepare(place, coarse_qkv, coarse_proj.T, coarse_up, coarse_down.T)
    tokens, theirs = lax.optimization_barrier((fine_tokens, theirs))
    normed = norm(tokens)
    got = core_swap(theirs)
    devices = lax.axis_size(AXES)
    up_one = [(i, (i + 1) % devices) for i in range(devices)]
    low = lax.ppermute(normed[-WIN:], AXES, up_one)
    high = lax.ppermute(normed[:WIN], AXES, [(b, a) for a, b in up_one])
    blocks = jnp.where(
        core == 0, jnp.concatenate([mine, got], axis=1), jnp.concatenate([got, mine], axis=1)
    )

    qu, d = arrange(place, direct(blocks, ("x", "z")))
    qu_one, qu_other = (hopped(qu, ("y", "y"), (step, -step)) for step in (1, -1))
    d_near = [d] + [hopped(d, ("z", "x"), (step, step)) for step in (1, -1)]

    qu, low, high, normed = lax.optimization_barrier((qu, low, high, normed))
    mid = fine_attention(fine_shift, fine_tokens, normed, low, high, fine_qkv, fine_proj)

    qu_one, qu_other, d_near, mid = lax.optimization_barrier((qu_one, qu_other, d_near, mid))
    qu_far = hopped(qu_one, ("y", "y"), (1, -1))
    d_far = hopped(d_near[0], ("z", "x"), (2, 2))
    skip, coarse = fine_mlp(place, window_counts, mid, fine_up, fine_down, merge_weight, out_weight)

    qu_far, d_far, coarse = lax.optimization_barrier((qu_far, d_far, coarse))
    qu_all = (qu, qu_one, qu_other, qu_far)
    q_two, u_two = jnp.stack([v[:, :128] for v in qu_all]), jnp.stack([v[:, 128:] for v in qu_all])
    d_two = jnp.stack([*d_near, d_far])
    q_one, q_other, q_far = (hopped(q_two, ("z", "x"), (step, step)) for step in (1, -1, 2))
    d_one = hopped(d_two, ("y", "y"), (1, -1))
    other = core_swap(coarse)
    other, u_two, d_late = lax.optimization_barrier((other, u_two, d_two))
    d_other = hopped(d_late, ("y", "y"), (-1, 1))
    u_parts = direct(u_two, ("z", "x"))
    q_far, d_one = lax.optimization_barrier((q_far, d_one))
    d_far = hopped(d_one, ("y", "y"), (1, -1))
    sent = coarse_attention(place, coarse, other, (q_two, q_one, q_other, q_far))
    came = core_swap(sent)
    base, give = coarse_mlp(
        place, coarse, other, sent, came, u_parts, (d_two, d_one, d_other, d_far)
    )
    return tail(base, core_swap(give), skip, expand_weight, out_weight)


def solution(mesh):
    wide = Mesh(mesh.devices.reshape(2, 4, 2, 2, 4), AXES)
    region, head = ("ylo", "z", "core"), ("yhi", "x")
    in_specs = (
        P(AXES, None),
        P(),
        P(region),
        P(),
        P(),
        P(),
        P(),
        P(),
        P(region, head),
        P(head, region),
        P(region, head),
        P(head, region),
        P(),
        P(),
    )
    return jax.shard_map(body, mesh=wide, in_specs=in_specs, out_specs=P(AXES, None), check_vma=False)
```

```python
import jax
import jax.numpy as jnp
from jax import lax
from jax.experimental import pallas as pl
from jax.experimental.pallas import tpu as pltpu
from jax.sharding import Mesh, PartitionSpec as P

C = 512
HD = 64
HF = 8
HC = 16
WIN = 144
AXES = ("ylo", "z", "core", "yhi", "x")
STEPS = (0, 1, -1, 2)
F32 = jnp.float32
BF16 = jnp.bfloat16
MIB = 1024 * 1024


def hopped(value, dims, steps):
    pairs = []
    for source in range(128):
        rest, here = source, {}
        for name, size in (("x", 4), ("yhi", 2), ("core", 2), ("z", 4), ("ylo", 2)):
            here[name] = rest % size
            rest //= size
        there = {"x": here["x"], "y": here["yhi"] * 2 + here["ylo"], "z": here["z"]}
        core = here["core"]
        there[dims[core]] = (there[dims[core]] + steps[core]) % 4
        ylo, yhi = there["y"] % 2, there["y"] // 2
        pairs.append((source, (((ylo * 4 + there["z"]) * 2 + core) * 2 + yhi) * 4 + there["x"]))
    return lax.ppermute(value, AXES, pairs)


def direct(value, dims):
    return [value if step == 0 else hopped(value, dims, (step, step)) for step in STEPS]


def core_swap(value):
    return lax.ppermute(value, "core", [(0, 1), (1, 0)])


def normalised(values):
    average = jnp.mean(values, axis=-1, keepdims=True)
    centred = values - average
    spread_of = jnp.mean(centred * centred, axis=-1, keepdims=True)
    return centred * lax.rsqrt(spread_of + 1e-05)


def gelu(hidden):
    return 0.5 * hidden * (1.0 + lax.erf(hidden * (0.5**0.5)))


def dot(a, b):
    return lax.dot_general(a, b, (((1,), (0,)), ((), ())), preferred_element_type=F32)


def dot_t(a, b):
    return lax.dot_general(a, b, (((1,), (1,)), ((), ())), preferred_element_type=F32)


def attend(packed, count):
    queries = packed[:, :HD] * jnp.asarray(HD ** (-0.5), BF16)
    keys = packed[:, HD : 2 * HD]
    values = packed[:, 2 * HD :]
    scores = dot_t(queries, keys)
    if count is not None:
        position = lax.broadcasted_iota(jnp.int32, scores.shape, 1)
        scores = jnp.where(position < count, scores, -1e30)
    row_max = jnp.max(scores, axis=-1, keepdims=True)
    raised = jnp.exp(scores - row_max)
    total = jnp.sum(raised, axis=-1, keepdims=True)
    return (dot(raised.astype(BF16), values) * (1.0 / total)).astype(BF16)


def vmem(count):
    return [pl.BlockSpec(memory_space=pltpu.VMEM)] * count


def cost(us):
    return pl.CostEstimate(flops=int(us * 1_150_000_000), bytes_accessed=0, transcendentals=0)


def params(mib):
    return pltpu.CompilerParams(vmem_limit_bytes=mib * MIB)


def norm_kernel(tokens, normed):
    normed[...] = normalised(tokens[...]).astype(BF16)


def norm(tokens):
    return pl.pallas_call(
        norm_kernel,
        out_shape=jax.ShapeDtypeStruct(tokens.shape, BF16),
        in_specs=vmem(1),
        out_specs=pl.BlockSpec(memory_space=pltpu.VMEM),
        compiler_params=params(8),
        cost_estimate=cost(1.0),
        name="norm",
    )(tokens)


def prepare_kernel(place, *refs):
    sources, (mine, theirs), held, sems = refs[:4], refs[4:6], refs[6:10], refs[10]
    copies = [
        pltpu.make_async_copy(source, target, sems.at[i])
        for i, (source, target) in enumerate(zip(sources, held))
    ]
    for copy in copies:
        copy.start()
    for copy in copies:
        copy.wait()
    qkv, proj_t, up, down_t = held
    halves = [
        (
            jnp.concatenate(
                [qkv[:, 192 * c : 192 * (c + 1)], proj_t[:, HD * c : HD * (c + 1)]], axis=1
            ),
            up[:, 256 * c : 256 * (c + 1)],
            down_t[:, 256 * c : 256 * (c + 1)],
        )
        for c in range(2)
    ]
    for core in range(2):

        @pl.when(place[3] == core)
        def _():
            for unit in range(3):
                mine[unit] = halves[core][unit]
                theirs[unit] = halves[1 - core][unit]


def prepare(place, qkv, proj_t, up, down_t):
    part = jax.ShapeDtypeStruct((3, 64, 256), BF16)
    arrays = (qkv, proj_t, up, down_t)
    return pl.pallas_call(
        prepare_kernel,
        out_shape=(part, part),
        in_specs=[pl.BlockSpec(memory_space=pltpu.SMEM)]
        + [pl.BlockSpec(memory_space=pltpu.HBM)] * 4,
        out_specs=tuple(vmem(2)),
        scratch_shapes=[pltpu.VMEM(v.shape, v.dtype) for v in arrays]
        + [pltpu.SemaphoreType.DMA((4,))],
        compiler_params=params(60),
        cost_estimate=cost(1.5),
        name="prepare",
    )(place, *arrays)


UP = 96


def arrange_kernel(place, own, r1, r2, r3, turned, down):
    here = jnp.where(place[3] == 0, place[0], place[2])
    for part, step in zip((own, r1, r2, r3), STEPS):
        at = along(here, -step)
        turned[at, :128] = part[0]
        turned[at, 128:] = part[1, :UP]
        down[at, :128] = part[2]
        down[at, 128:] = part[1, UP:]


def arrange(place, parts):
    return pl.pallas_call(
        arrange_kernel,
        out_shape=(
            jax.ShapeDtypeStruct((4, 128 + UP, 256), BF16),
            jax.ShapeDtypeStruct((4, 256 - UP, 256), BF16),
        ),
        in_specs=[pl.BlockSpec(memory_space=pltpu.SMEM)] + vmem(4),
        out_specs=tuple(vmem(2)),
        compiler_params=params(6),
        cost_estimate=cost(0.7),
        name="arrange",
    )(place, *parts)


def along(i, step):
    return lax.rem(i + step + 4, 4)


def fine_attention_kernel(offset, tokens, normed, low, high, qkv, proj, out, ext, packed, blend):
    rows = normed.shape[0]
    shift = offset[0]
    ext[0:WIN, :] = low[...].astype(F32)
    ext[WIN : WIN + rows, :] = normed[...].astype(F32)
    ext[WIN + rows :, :] = high[...].astype(F32)
    rolled = pltpu.roll(ext[...], ext.shape[0] - shift, 0)[: rows + WIN].astype(BF16)
    packed[...] = dot(rolled, qkv[...]).astype(BF16)

    def window(w, carry):
        start = pl.multiple_of(w * WIN, WIN)
        for head in range(HF):
            part = packed[pl.ds(start, WIN), head * 3 * HD : (head + 1) * 3 * HD]
            blend[pl.ds(start, WIN), head * HD : (head + 1) * HD] = attend(part, None)
        return carry

    lax.fori_loop(0, (rows + WIN) // WIN, window, 0)
    ext[0 : rows + WIN, :] = dot(blend[...], proj[...])
    back = pltpu.roll(ext[...], shift + rows + WIN, 0)
    out[...] = tokens[...] + back[:rows]


def fine_attention(offset, tokens, normed, low, high, qkv, proj):
    rows = tokens.shape[0]
    return pl.pallas_call(
        fine_attention_kernel,
        out_shape=jax.ShapeDtypeStruct((rows, C), F32),
        in_specs=[pl.BlockSpec(memory_space=pltpu.SMEM)] + vmem(6),
        out_specs=pl.BlockSpec(memory_space=pltpu.VMEM),
        scratch_shapes=[
            pltpu.VMEM((rows + 2 * WIN, C), F32),
            pltpu.VMEM((rows + WIN, 3 * C), BF16),
            pltpu.VMEM((rows + WIN, C), BF16),
        ],
        compiler_params=params(26),
        cost_estimate=pl.CostEstimate(flops=2_500_000_000, bytes_accessed=6_000_000, transcendentals=900_000),
        name="fine_attention",
    )(offset, tokens, normed, low, high, qkv, proj)


def fine_mlp_kernel(place, counts, mid, up, down, merge, out_weight, skip, coarse, total, lanes):
    rows = mid.shape[0]
    fine = normalised(mid[...]).astype(BF16)
    total[...] = mid[...]
    for part in range(4):
        hidden = gelu(dot(fine, up[:, part * C : (part + 1) * C])).astype(BF16)
        total[...] += dot(hidden, down[part * C : (part + 1) * C, :])
    skip[...] = dot(total[...].astype(BF16), out_weight[:C, :])
    for k in range(4):
        lanes[k] = total[:, k * 128 : (k + 1) * 128]
    pieces = [
        jnp.concatenate([lanes[k, pl.ds(j, rows // 4, stride=4), :] for k in range(4)], axis=1)
        for j in range(4)
    ]
    average = sum(jnp.sum(p, axis=-1, keepdims=True) for p in pieces) * (1.0 / (4 * C))
    pieces = [p - average for p in pieces]
    square = sum(jnp.sum(p * p, axis=-1, keepdims=True) for p in pieces) * (1.0 / (4 * C))
    scale = lax.rsqrt(square + 1e-05)
    result = None
    for j, p in enumerate(pieces):
        term = dot((p * scale).astype(BF16), merge[j * C : (j + 1) * C, :])
        result = term if result is None else result + term
    coarse[:WIN, :] = result
    count = counts[place[1] // 2 * 4 + place[0]]
    coarse[WIN:, :] = jnp.full((8, 2 * C), count, jnp.int32).astype(F32)


def fine_mlp(place, counts, mid, up, down, merge, out_weight):
    rows = mid.shape[0]
    return pl.pallas_call(
        fine_mlp_kernel,
        out_shape=(
            jax.ShapeDtypeStruct((rows, C), F32),
            jax.ShapeDtypeStruct((rows // 4 + 8, 2 * C), F32),
        ),
        in_specs=[pl.BlockSpec(memory_space=pltpu.SMEM)] * 2 + vmem(5),
        out_specs=tuple(vmem(2)),
        scratch_shapes=[pltpu.VMEM((rows, C), F32), pltpu.VMEM((4, rows, 128), F32)],
        compiler_params=params(32),
        cost_estimate=pl.CostEstimate(flops=3_500_000_000, bytes_accessed=12_000_000, transcendentals=1_200_000),
        name="fine_mlp",
    )(place, counts, mid, up, down, merge, out_weight)


def fetch(place, pieces, weight, sems, first=0):
    zeros, ones = [], []
    for at, (source, y, z, x) in enumerate(pieces):
        yhi, ylo = lax.div(y, 2), lax.rem(y, 2)
        rows = pl.ds(first, source.shape[1])
        zeros.append(
            pltpu.make_async_copy(source, weight.at[yhi, :, ylo, z, rows], sems.at[at])
        )
        ones.append(
            pltpu.make_async_copy(source, weight.at[yhi, x, ylo, :, rows], sems.at[at])
        )

    @pl.when(place[3] == 0)
    def _():
        for copy in zeros:
            copy.start()

    @pl.when(place[3] == 1)
    def _():
        for copy in ones:
            copy.start()

    return zeros


def fetch_turned(place, parts, weight, sems):
    x, y, z = place[0], place[1], place[2]
    turn = 1 - 2 * place[3]
    return fetch(
        place,
        [
            (parts[at].at[slot], along(y, step), along(z, -STEPS[at]), along(x, -STEPS[at]))
            for at in range(4)
            for slot, step in enumerate((0, -turn, turn, 2))
        ],
        weight,
        sems,
    )


def fetch_down(place, parts, rows, weight, sems, first=0):
    x, y, z = place[0], place[1], place[2]
    turn = 1 - 2 * place[3]
    return fetch(
        place,
        [
            (part.at[slot, :, rows], along(y, step), along(z, -STEPS[slot]), along(x, -STEPS[slot]))
            for part, step in zip(parts, (0, -turn, turn, 2))
            for slot in range(4)
        ],
        weight,
        sems,
        first,
    )


def whole(weight, head):
    return weight[head // 4, head % 4].reshape(2 * C, 256)


def coarse_attention_kernel(place, own, other, a0, a1, a2, a3, out, weight, x, blend, proj, sems):
    copies = fetch_turned(place, (a0, a1, a2, a3), weight, sems)
    x[:WIN, :] = normalised(own[:WIN, :]).astype(BF16)
    x[WIN:, :] = normalised(other[:WIN, :]).astype(BF16)
    counts = [part[WIN : WIN + 1, :1].astype(jnp.int32) for part in (own, other)]
    for copy in copies:
        copy.wait()
    for head in range(8):
        both = whole(weight, head)
        packed = dot(x[...], both[:, : 3 * HD]).astype(BF16)
        for w in range(2):
            blend[w * WIN : (w + 1) * WIN, head * HD : (head + 1) * HD] = attend(
                packed[w * WIN : (w + 1) * WIN], counts[w]
            )
        proj[:, head * HD : (head + 1) * HD] = both[:, 3 * HD :]
    out[...] = dot_t(blend[...], proj[...]).astype(BF16).reshape(out.shape)


def coarse_attention(place, own, other, parts):
    return pl.pallas_call(
        coarse_attention_kernel,
        out_shape=jax.ShapeDtypeStruct((2, WIN, 2 * C), BF16),
        in_specs=[pl.BlockSpec(memory_space=pltpu.SMEM)]
        + vmem(2)
        + [pl.BlockSpec(memory_space=pl.ANY)] * 4,
        out_specs=pl.BlockSpec(memory_space=pltpu.VMEM),
        scratch_shapes=[
            pltpu.VMEM((2, 4, 2, 4, 128, 256), BF16),
            pltpu.VMEM((2 * WIN, 2 * C), BF16),
            pltpu.VMEM((2 * WIN, C), BF16),
            pltpu.VMEM((2 * C, C), BF16),
            pltpu.SemaphoreType.DMA((16,)),
        ],
        compiler_params=params(24),
        cost_estimate=pl.CostEstimate(flops=1_400_000_000, bytes_accessed=7_000_000, transcendentals=400_000),
        name="coarse_attention",
    )(place, own, other, *parts)


def coarse_mlp_kernel(
    place, own, other, sent, came, u0, u1, u2, u3, d0, d1, d2, d3, base, give, up, down, x, hid, sems, rest_sems, late_sems
):
    copies = fetch_turned(place, (u0, u1, u2, u3), up, sems)
    downs = (d0, d1, d2, d3)
    copies += fetch_down(place, downs, pl.ds(128, 128 - UP), up, rest_sems, UP)
    mid = own[:WIN, :] + (sent[0].astype(F32) + came[1].astype(F32))
    base[...] = mid
    x[:WIN, :] = normalised(mid).astype(BF16)
    x[WIN:, :] = normalised(other[:WIN, :] + (sent[1].astype(F32) + came[0].astype(F32))).astype(BF16)
    late = fetch_down(place, downs, pl.ds(0, 128), down, late_sems)
    for copy in copies:
        copy.wait()
    for h in range(8):
        hid[h] = gelu(dot(x[...], whole(up, h))).astype(BF16)
    for copy in late:
        copy.wait()
    for chunk in range(4):
        ylo, z = chunk // 2, chunk % 2 * 2
        result = None
        for h in range(8):
            block = down[h // 4, h % 4, ylo, z : z + 2].reshape(256, 256)
            term = dot_t(hid[h], block)
            result = term if result is None else result + term
        at = slice(chunk * 256, (chunk + 1) * 256)
        base[:, at] += result[:WIN]
        give[:, at] = result[WIN:].astype(BF16)


def coarse_mlp(place, own, other, sent, came, ups, downs):
    return pl.pallas_call(
        coarse_mlp_kernel,
        out_shape=(
            jax.ShapeDtypeStruct((WIN, 2 * C), F32),
            jax.ShapeDtypeStruct((WIN, 2 * C), BF16),
        ),
        in_specs=[pl.BlockSpec(memory_space=pltpu.SMEM)]
        + vmem(4)
        + [pl.BlockSpec(memory_space=pl.ANY)] * 8,
        out_specs=tuple(vmem(2)),
        scratch_shapes=[
            pltpu.VMEM((2, 4, 2, 4, 128, 256), BF16),
            pltpu.VMEM((2, 4, 2, 4, 128, 256), BF16),
            pltpu.VMEM((2 * WIN, 2 * C), BF16),
            pltpu.VMEM((8, 2 * WIN, 256), BF16),
            pltpu.SemaphoreType.DMA((16,)),
            pltpu.SemaphoreType.DMA((16,)),
            pltpu.SemaphoreType.DMA((16,)),
        ],
        compiler_params=params(32),
        cost_estimate=pl.CostEstimate(flops=2_400_000_000, bytes_accessed=14_000_000, transcendentals=600_000),
        name="coarse_mlp",
    )(place, own, other, sent, came, *ups, *downs)


def tail_kernel(base, came, skip, expand, out_weight, out, lanes):
    coarse_out = (base[...] + came[...].astype(F32)).astype(BF16)
    for j in range(4):
        rows = dot(coarse_out, expand[:, j * C : (j + 1) * C]).astype(BF16)
        spread_rows = dot(rows, out_weight[C:, :])
        for k in range(4):
            lanes[k, pl.ds(j, WIN, stride=4), :] = spread_rows[:, k * 128 : (k + 1) * 128]
    for k in range(4):
        at = slice(k * 128, (k + 1) * 128)
        out[:, at] = skip[:, at] + lanes[k]


def tail(base, came, skip, expand, out_weight):
    return pl.pallas_call(
        tail_kernel,
        out_shape=jax.ShapeDtypeStruct(skip.shape, F32),
        in_specs=vmem(5),
        out_specs=pl.BlockSpec(memory_space=pltpu.VMEM),
        scratch_shapes=[pltpu.VMEM((4, skip.shape[0], 128), F32)],
        compiler_params=params(20),
        cost_estimate=pl.CostEstimate(flops=900_000_000, bytes_accessed=8_000_000, transcendentals=0),
        name="tail",
    )(base, came, skip, expand, out_weight)


def body(
    fine_tokens,
    fine_shift,
    window_counts,
    fine_qkv,
    fine_proj,
    fine_up,
    fine_down,
    merge_weight,
    coarse_qkv,
    coarse_proj,
    coarse_up,
    coarse_down,
    expand_weight,
    out_weight,
):
    core = lax.axis_index("core")
    y = lax.axis_index("yhi") * 2 + lax.axis_index("ylo")
    place = jnp.stack([lax.axis_index("x"), y, lax.axis_index("z"), core]).astype(jnp.int32)
    mine, theirs = prepare(place, coarse_qkv, coarse_proj.T, coarse_up, coarse_down.T)
    tokens, theirs = lax.optimization_barrier((fine_tokens, theirs))
    normed = norm(tokens)
    got = core_swap(theirs)
    devices = lax.axis_size(AXES)
    up_one = [(i, (i + 1) % devices) for i in range(devices)]
    low = lax.ppermute(normed[-WIN:], AXES, up_one)
    high = lax.ppermute(normed[:WIN], AXES, [(b, a) for a, b in up_one])
    blocks = jnp.where(
        core == 0, jnp.concatenate([mine, got], axis=1), jnp.concatenate([got, mine], axis=1)
    )

    qu, d = arrange(place, direct(blocks, ("x", "z")))
    qu_one, qu_other = (hopped(qu, ("y", "y"), (step, -step)) for step in (1, -1))
    d_near = [d] + [hopped(d, ("z", "x"), (step, step)) for step in (1, -1)]

    qu, low, high, normed = lax.optimization_barrier((qu, low, high, normed))
    mid = fine_attention(fine_shift, fine_tokens, normed, low, high, fine_qkv, fine_proj)

    qu_one, qu_other, d_near, mid = lax.optimization_barrier((qu_one, qu_other, d_near, mid))
    qu_far = hopped(qu_one, ("y", "y"), (1, -1))
    d_far = hopped(d_near[0], ("z", "x"), (2, 2))
    skip, coarse = fine_mlp(place, window_counts, mid, fine_up, fine_down, merge_weight, out_weight)

    qu_far, d_far, coarse = lax.optimization_barrier((qu_far, d_far, coarse))
    qu_all = (qu, qu_one, qu_other, qu_far)
    q_two, u_two = jnp.stack([v[:, :128] for v in qu_all]), jnp.stack([v[:, 128:] for v in qu_all])
    d_two = jnp.stack([*d_near, d_far])
    q_one, q_other, q_far = (hopped(q_two, ("z", "x"), (step, step)) for step in (1, -1, 2))
    d_one = hopped(d_two, ("y", "y"), (1, -1))
    other = core_swap(coarse)
    other, u_two, d_late = lax.optimization_barrier((other, u_two, d_two))
    d_other = hopped(d_late, ("y", "y"), (-1, 1))
    u_parts = direct(u_two, ("z", "x"))
    q_far, d_one = lax.optimization_barrier((q_far, d_one))
    d_far = hopped(d_one, ("y", "y"), (1, -1))
    sent = coarse_attention(place, coarse, other, (q_two, q_one, q_other, q_far))
    came = core_swap(sent)
    base, give = coarse_mlp(
        place, coarse, other, sent, came, u_parts, (d_two, d_one, d_other, d_far)
    )
    return tail(base, core_swap(give), skip, expand_weight, out_weight)


def solution(mesh):
    wide = Mesh(mesh.devices.reshape(2, 4, 2, 2, 4), AXES)
    region, head = ("ylo", "z", "core"), ("yhi", "x")
    in_specs = (
        P(AXES, None),
        P(),
        P(region),
        P(),
        P(),
        P(),
        P(),
        P(),
        P(region, head),
        P(head, region),
        P(region, head),
        P(head, region),
        P(),
        P(),
    )
    return jax.shard_map(body, mesh=wide, in_specs=in_specs, out_specs=P(AXES, None), check_vma=False)
```
